32 devices in a mesh: section: 4 (over x, core), expert: 4 (over z), tensor: 2 (over y).
Axes of the slice: x: 2, y: 2, z: 4, core: 2. Of those that a mesh axis runs over, the one named last changes fastest.
Arguments:
- tokens: bfloat16 [2048, 5120], P(('section', 'expert'), 'tensor'), may hold values from -6 to 6
- norm_gain: float32 [5120], P('tensor'), may hold values from 0.1 to 1.9
- router: bfloat16 [5120, 4], P('tensor'), may hold values from -0.078125 to 0.078125
- expert_ids: int32 [2048, 1], P(('section', 'expert')), may hold values from 0 to 3; in each aligned block of 128 rows (0 to 127, 128 to 255, ...) at most 64 rows name the same one
- gate_proj: bfloat16 [4, 5120, 4096], P('expert', None, ('section', 'tensor')), may hold values from -0.078125 to 0.078125
- up_proj: bfloat16 [4, 5120, 4096], P('expert', None, ('section', 'tensor')), may hold values from -0.078125 to 0.078125
- down_proj: bfloat16 [4, 4096, 5120], P('expert', 'section', 'tensor'), may hold values from -0.09375 to 0.09375
Outputs:
- moe_out: bfloat16 [2048, 5120], P(('section', 'expert'), 'tensor')
The draws below stay inside these ranges and needn't reach their ends.
Inputs may be any that keep to these rules, and one draw needn't show every extreme that they name: `expert_ids`: within each aligned block of 128 tokens (the tokens of one group of devices along section and expert) no expert is named by more than 64 tokens, a bound that some block reaches.
All inputs are finite; a program needn't handle non-finite values.
Results may differ from the reference program's by a relative error of at most 0.017.
Values may be sent and summed in bfloat16 or wider, within the bound.
A program may use at most 64 MiB of HBM per device.

```python
import math
from functools import partial
import jax
import jax.numpy as jnp
import numpy as np
from jax import lax

D = 5120
HE = 4096
TOK_DEV = 128
EXPERTS = 4
CAP = 64
TOKENS = 2048


def steps_of(own_key, extent, shards, low, high):
    level = 1.0
    for position, parts in shards:
        heights = jax.random.uniform(jax.random.fold_in(jax.random.fold_in(own_key, 6), position), (parts,), jnp.float32, low / len(shards), high / len(shards))
        level = level * jnp.repeat(jnp.exp(heights), extent[position] // parts).reshape((-1,) + (1,) * (len(extent) - 1 - position))
    return level


def shared_out(rng, own, number, rows, number_of, top, limit, lean):
    order = jax.random.permutation(rng, number_of)
    heavy_load, ordinary = shares(number_of, rows * top, limit, lean, True), shares(number_of, rows * top, limit, lean, False)
    places = jnp.arange(number_of)

    def named(tallies, offset_by):
        used = int((tallies > 0).sum())
        fixed = max(1, used // 4)
        passed = fixed + (places - fixed + offset_by * (used - fixed)) % max(1, number_of - fixed)
        return jnp.zeros((number_of,), jnp.int32).at[order[jnp.where(places < fixed, places, passed)]].set(jnp.asarray(tallies, jnp.int32))

    tallies = jnp.where(number % 4 == 0, named(heavy_load, number // 4), named(ordinary, number - number // 4 - 1))
    mixed = jax.random.permutation(jax.random.fold_in(own, 3), number_of)
    donor, taker = mixed[0:number_of // 2 * 2:2], mixed[1:number_of // 2 * 2:2]
    room = jnp.minimum(tallies[donor] - 1, limit - tallies[taker]) // 2
    room = jnp.where((donor == order[0]) | (taker == order[0]) | (tallies[taker] == 0), 0, jnp.maximum(room, 0))
    passed = jax.random.randint(jax.random.fold_in(own, 4), (number_of // 2,), 0, 1 << 20) % (room + 1)
    tallies = tallies.at[donor].add(-passed).at[taker].add(passed)
    members = jnp.searchsorted(jnp.cumsum(tallies), jnp.arange(rows * top), side="right").astype(jnp.int32)
    grid = members.reshape(top, rows).T
    grid = grid[jax.random.permutation(jax.random.fold_in(own, 1), rows)]
    offset_by = jax.random.randint(jax.random.fold_in(own, 2), (rows, 1), 0, top)
    return jnp.take_along_axis(grid, (jnp.arange(top)[None, :] + offset_by) % top, axis=1)


def shares(amount, total, reach, lean, full):
    loads = [(1 << 20) // math.isqrt(standing ** lean) + 1 for standing in range(1, amount + 1)]
    largest = reach if full else min(reach, max(-(-total // amount), total * loads[0] // sum(loads)))
    least = 1 if total - largest >= amount - 1 else 0
    counts, surplus = [largest] + [least] * (amount - 1), total - largest - least * (amount - 1)
    while surplus > 0:
        free = [i for i in range(1, amount) if counts[i] < largest] or [i for i in range(1, amount) if counts[i] < reach]
        pool, left = sum([loads[i] for i in free]), surplus
        for i in free:
            more = min(reach - counts[i], max(1, left * loads[i] // pool), surplus)
            counts[i] = counts[i] + more
            surplus = surplus - more
    return np.array(counts)


def centred(rng, shape, scale, limit, split=(), kind=jnp.bfloat16):
    values = scale * jax.random.normal(rng, shape, jnp.float32)
    if split:
        values = values * steps_of(rng, shape, split, -0.22, 0.18)
    return jnp.clip(values, -limit, limit).astype(kind)


def setup_inputs(seed: int = 0) -> dict:
    key_list = jax.random.split(jax.random.key(seed), 8)
    tokens = centred(key_list[0], (TOKENS, D), 1.0, 6.0, ((0, 16), (1, 2)))
    norm_gain = jnp.clip(1.0 + 0.18 * jax.random.normal(key_list[1], (D,), jnp.float32), 0.1, 1.9)
    router = centred(key_list[2], (D, EXPERTS), D ** -0.5, 0.078125, ((0, 2),))
    expert_ids_keys = jax.random.split(jax.random.fold_in(key_list[3], 1), TOKENS // TOK_DEV)
    expert_ids_turns = jax.random.permutation(jax.random.fold_in(key_list[3], 3), TOKENS // TOK_DEV)
    expert_ids = jax.vmap(lambda own, number: shared_out(jax.random.fold_in(key_list[3], 2), own, number, TOK_DEV, EXPERTS, 1, CAP, 2))(expert_ids_keys, expert_ids_turns).reshape((TOKENS, 1))
    gate_proj = centred(key_list[4], (EXPERTS, D, HE), D ** -0.5, 0.078125, ((0, 4), (2, 8)))
    up_proj = centred(key_list[5], (EXPERTS, D, HE), D ** -0.5, 0.078125, ((0, 4), (2, 8)))
    down_proj = centred(key_list[6], (EXPERTS, HE, D), HE ** -0.5, 0.09375, ((0, 4), (1, 4), (2, 2)))
    return dict(tokens=tokens, norm_gain=norm_gain, router=router, expert_ids=expert_ids, gate_proj=gate_proj, up_proj=up_proj, down_proj=down_proj)


EPSILON = 1e-05

def slot_table(expert_ids, experts, capacity):
    chosen = expert_ids[:, 0].astype(jnp.int32)
    member = (chosen[:, None] == jnp.arange(experts, dtype=jnp.int32)[None, :]).astype(jnp.int32)
    earlier = (jnp.cumsum(member, axis=0) - member).astype(jnp.int32)
    placed = (chosen * capacity + lax.optimization_barrier(jnp.sum(earlier * member, axis=1))).astype(jnp.int32)
    placing = placed[:, None] == jnp.arange(experts * capacity, dtype=jnp.int32)[None, :]
    return (member, placing)

def normalize(tokens, norm_gain, squares):
    values = tokens.astype(jnp.float32)
    return (values * lax.rsqrt(squares / D + EPSILON) * norm_gain).astype(jnp.bfloat16)

def expert_apply(inputs):
    rows, gate_w, up_w, down_w = inputs
    gate = jnp.dot(rows, gate_w, preferred_element_type=jnp.float32)
    upper = jnp.dot(rows, up_w, preferred_element_type=jnp.float32)
    hidden = (jax.nn.silu(gate) * upper).astype(jnp.bfloat16)
    return jnp.dot(hidden, down_w, preferred_element_type=jnp.float32).astype(jnp.bfloat16)

def reference(tokens, norm_gain, router, expert_ids, gate_proj, up_proj, down_proj):
    values = tokens.astype(jnp.float32)
    normed = normalize(tokens, norm_gain, lax.optimization_barrier(jnp.sum(values * values, axis=1, keepdims=True)))
    logits = jnp.dot(normed, router, preferred_element_type=jnp.float32)
    groups = tokens.shape[0] // TOK_DEV
    member, placing = jax.vmap(partial(slot_table, experts=EXPERTS, capacity=CAP))(expert_ids.reshape(groups, TOK_DEV, 1))
    member = member.reshape(groups * TOK_DEV, EXPERTS)
    score = jax.nn.sigmoid(lax.optimization_barrier(jnp.sum(jnp.where(member > 0, logits, jnp.float32(0.0)), axis=1)))
    routed = (normed.astype(jnp.float32) * score[:, None]).astype(jnp.bfloat16)
    routed = routed.reshape(groups, TOK_DEV, D)
    placing_f = placing.astype(jnp.float32)
    buffers = jnp.einsum('gtc,gtd->gcd', placing_f, routed.astype(jnp.float32)).astype(jnp.bfloat16)
    per_expert = buffers.reshape(groups, EXPERTS, CAP, D).transpose(1, 0, 2, 3).reshape(EXPERTS, groups * CAP, D)
    outputs = lax.map(expert_apply, (per_expert, gate_proj, up_proj, down_proj))
    back = outputs.reshape(EXPERTS, groups, CAP, D).transpose(1, 0, 2, 3).reshape(groups, EXPERTS * CAP, D)
    result = jnp.einsum('gtc,gcd->gtd', placing_f, back.astype(jnp.float32))
    return result.reshape(groups * TOK_DEV, D).astype(jnp.bfloat16)
```

```python
import functools

import jax
import jax.numpy as jnp
from jax import lax
from jax.experimental import pallas as pl
from jax.experimental.pallas import tpu as pltpu
from jax.sharding import PartitionSpec as P

EPSILON = 1e-05
CORES = 2
LANES = 128
MESH = pl.DeviceIdType.MESH


def tile_of(width):
    for tile in (512, 256, 128):
        if width % tile == 0:
            return tile
    return width


def sublayer(
    sections, experts, tensors, tokens_ref, gain_ref, router_ref, ids_ref, gate_hbm, up_hbm, down_hbm,
    out_ref, gate_w, up_w, down_w, stats, placing_ref, outgoing, piece, hidden, part, pair_in, cross_out,
    cross_in, back_out, back_in, weight_sem, stats_s, stats_r, out_s, piece_r, core_s, relay_s, px_s,
    pt_s, hid_s, hid_r, pair_s, pair_r, cross_s, cross_r, back_s, back_r,
):
    s, e, t = lax.axis_index("section"), lax.axis_index("expert"), lax.axis_index("tensor")
    x, c = lax.div(s, CORES), lax.rem(s, CORES)
    xs = sections // CORES
    rows, feats = tokens_ref.shape
    width = gate_hbm.shape[1]
    units = gate_hbm.shape[2]
    cap = outgoing.shape[0] // experts
    partner = s + 1 - 2 * c

    def other_x(k):
        return lax.rem(x + k, xs)

    def other_t(k):
        return lax.rem(t + k, tensors)

    def sec(xx, cc):
        return xx * CORES + cc

    def dev(ss, ee, tt):
        return {"section": ss, "expert": ee, "tensor": tt}

    barrier = pltpu.get_barrier_semaphore()
    peers = [dev(partner, e, t)]
    peers += [dev(sec(other_x(k), c), e, t) for k in range(1, xs)]
    peers += [dev(s, e, other_t(k)) for k in range(1, tensors)]
    peers += [dev(s, lax.rem(e + k, experts), t) for k in range(1, experts)]
    for peer in peers:
        pl.semaphore_signal(barrier, inc=1, device_id=peer, device_id_type=MESH)

    loads = [
        pltpu.make_async_copy(gate_hbm.at[0], gate_w, weight_sem.at[0]),
        pltpu.make_async_copy(up_hbm.at[0], up_w, weight_sem.at[1]),
        pltpu.make_async_copy(down_hbm.at[0], down_w, weight_sem.at[2]),
    ]
    for load in loads:
        load.start()

    ft = tile_of(feats)

    def span(n, tile):
        return pl.ds(pl.multiple_of(n * tile, LANES), tile)

    def gather_stats(n, carry):
        squares, logits = carry
        values = tokens_ref[:, span(n, ft)].astype(jnp.float32)
        scaled = (values * gain_ref[:, span(n, ft)]).astype(jnp.bfloat16)
        logits += jnp.dot(
            scaled, router_ref[pl.ds(pl.multiple_of(n * ft, LANES), ft), :],
            preferred_element_type=jnp.float32,
        )
        return squares + jnp.sum(values * values, axis=1, keepdims=True), logits

    squares, logits = lax.fori_loop(
        0, feats // ft, gather_stats,
        (jnp.zeros((rows, 1), jnp.float32), jnp.zeros((rows, LANES), jnp.float32)),
    )
    lane = lax.broadcasted_iota(jnp.int32, (rows, LANES), 1)
    stats[t] = jnp.where(lane == experts, squares, logits)
    pl.semaphore_wait(barrier, len(peers))

    def stats_copy(k):
        return pltpu.make_async_remote_copy(
            stats.at[t], stats.at[t], stats_s.at[k], stats_r.at[t],
            device_id=dev(s, e, other_t(k)), device_id_type=MESH,
        )

    for k in range(1, tensors):
        stats_copy(k).start()

    chosen = ids_ref[...]
    member = chosen == lane
    member_f = jnp.where(member, 1.0, 0.0).astype(jnp.float32)
    before = (
        lax.broadcasted_iota(jnp.int32, (rows, rows), 1) < lax.broadcasted_iota(jnp.int32, (rows, rows), 0)
    )
    earlier = jnp.dot(
        jnp.where(before, 1.0, 0.0).astype(jnp.bfloat16), member_f.astype(jnp.bfloat16),
        preferred_element_type=jnp.float32,
    )
    slot = jnp.sum(earlier * member_f, axis=1, keepdims=True)
    placed = chosen.astype(jnp.float32) * cap + slot
    places = lax.broadcasted_iota(jnp.int32, (rows, experts * cap), 1).astype(jnp.float32)
    placing_ref[...] = jnp.where(placed == places, 1.0, 0.0).astype(jnp.bfloat16)

    for k in range(1, tensors):
        pltpu.make_async_remote_copy(
            stats.at[t], stats.at[other_t(k)], stats_s.at[k], stats_r.at[other_t(k)],
            device_id=dev(s, e, other_t(k)), device_id_type=MESH,
        ).wait_recv()
    total = stats[0]
    for k in range(1, tensors):
        total += stats[k]
    squares = jnp.sum(jnp.where(lane == experts, total, 0.0), axis=1, keepdims=True)
    inverse = lax.rsqrt(squares / width + EPSILON)
    score = jax.nn.sigmoid(jnp.sum(total * member_f, axis=1, keepdims=True) * inverse)

    @pl.loop(0, feats // ft)
    def _(n):
        values = tokens_ref[:, span(n, ft)].astype(jnp.float32)
        normed = (values * inverse * gain_ref[:, span(n, ft)]).astype(jnp.bfloat16)
        routed = (normed.astype(jnp.float32) * score).astype(jnp.bfloat16)
        outgoing[:, span(n, ft)] = lax.dot_general(
            placing_ref[...], routed, (((0,), (0,)), ((), ())), preferred_element_type=jnp.float32
        ).astype(jnp.bfloat16)

    def group_rows(index):
        return pl.ds(pl.multiple_of(index * cap, cap), cap)

    def block(z, ss, tt):
        return piece.at[z, group_rows(ss), pl.ds(pl.multiple_of(tt * feats, LANES), feats)]

    def chunk_copy(z, ss, tt, send_sem, to):
        return pltpu.make_async_remote_copy(
            block(z, ss, tt), block(z, ss, tt), send_sem, piece_r.at[z, ss, tt],
            device_id=to, device_id_type=MESH,
        )

    def out_copy(k):
        target = lax.rem(e + k, experts)
        return pltpu.make_async_remote_copy(
            outgoing.at[group_rows(target)], block(e, s, t), out_s.at[k], piece_r.at[e, s, t],
            device_id=dev(s, target, t), device_id_type=MESH,
        )

    own = pltpu.make_async_copy(outgoing.at[group_rows(e)], block(e, s, t), piece_r.at[e, s, t])
    own.start()
    for k in range(1, experts):
        out_copy(k).start()

    def source(i):
        return lax.rem(e + experts - i, experts)

    to_partner = dev(partner, e, t)

    def arrived(z, ss, tt):
        chunk_copy(z, ss, tt, core_s.at[0, 0, 0], to_partner).wait_recv()

    def core_copy(i, xx, tt):
        return chunk_copy(source(i), sec(xx, c), tt, core_s.at[i, xx, tt], to_partner)

    def px_copy(i, k):
        return chunk_copy(source(i), s, t, px_s.at[i, k], dev(sec(other_x(k), c), e, t))

    def pt_copy(i, k):
        return chunk_copy(source(i), s, t, pt_s.at[i, k], dev(s, e, other_t(k)))

    def relay_t_copy(i, kx, kt):
        return chunk_copy(
            source(i), sec(other_x(kx), c), t, relay_s.at[i, kx, kt], dev(s, e, other_t(kt))
        )

    def relay_x_copy(i, kx, kt):
        return chunk_copy(
            source(i), s, other_t(kt), relay_s.at[i, kx, kt], dev(sec(other_x(kx), c), e, t)
        )

    def push(i):
        arrived(source(i), s, t)
        for k in range(1, xs):
            px_copy(i, k).start()
        for k in range(1, tensors):
            pt_copy(i, k).start()
        core_copy(i, x, t).start()

    def relay(i):
        even = lax.rem(i, 2) == 0
        for kx in range(1, xs):
            arrived(source(i), sec(other_x(kx), c), t)

            @pl.when(even)
            def _():
                for kt in range(1, tensors):
                    relay_t_copy(i, kx, kt).start()

            core_copy(i, other_x(kx), t).start()
        for kt in range(1, tensors):
            arrived(source(i), s, other_t(kt))

            @pl.when(jnp.logical_not(even))
            def _():
                for kx in range(1, xs):
                    relay_x_copy(i, kx, kt).start()

            core_copy(i, x, other_t(kt)).start()

    def hid_block(i, tt):
        return hidden.at[i, :, pl.ds(pl.multiple_of(tt * units, LANES), units)]

    def hid_copy(i, k):
        return pltpu.make_async_remote_copy(
            hid_block(i, t), hid_block(i, t), hid_s.at[i, k], hid_r.at[i, t],
            device_id=dev(s, e, other_t(k)), device_id_type=MESH,
        )

    ut = min(256, units)

    def expand(i):
        z = source(i)
        for kx in range(1, xs):
            for kt in range(1, tensors):
                arrived(z, sec(other_x(kx), c), other_t(kt))
                core_copy(i, other_x(kx), other_t(kt)).start()
        for xx in range(xs):
            for tt in range(tensors):
                arrived(z, sec(xx, 1 - c), tt)

        @pl.when(i == 0)
        def _():
            loads[0].wait()
            loads[1].wait()
            loads[2].wait()

        @pl.loop(0, units // ut)
        def _(n):
            gate = jnp.dot(piece[z], gate_w[:, span(n, ut)], preferred_element_type=jnp.float32)
            upper = jnp.dot(piece[z], up_w[:, span(n, ut)], preferred_element_type=jnp.float32)
            hidden[i, :, pl.ds(pl.multiple_of(t * units + n * ut, LANES), ut)] = (
                jax.nn.silu(gate) * upper
            ).astype(jnp.bfloat16)

        for k in range(1, tensors):
            hid_copy(i, k).start()

    def pair_copy(i, xx):
        return pltpu.make_async_remote_copy(
            part.at[i, group_rows(sec(xx, 1 - c))], pair_in.at[i, xx], pair_s.at[i, xx], pair_r.at[i, xx],
            device_id=to_partner, device_id_type=MESH,
        )

    def contract(i):
        for k in range(1, tensors):
            pltpu.make_async_remote_copy(
                hid_block(i, t), hid_block(i, other_t(k)), hid_s.at[i, k], hid_r.at[i, other_t(k)],
                device_id=dev(s, e, other_t(k)), device_id_type=MESH,
            ).wait_recv()

        @pl.loop(0, feats // ft)
        def _(n):
            part[i, :, span(n, ft)] = jnp.dot(
                hidden[i], down_w[:, span(n, ft)], preferred_element_type=jnp.float32
            ).astype(jnp.bfloat16)

        for xx in range(xs):
            pair_copy(i, xx).start()

    def cross_copy(i, k):
        return pltpu.make_async_remote_copy(
            cross_out.at[i, k - 1], cross_in.at[i, k - 1], cross_s.at[i, k], cross_r.at[i, k],
            device_id=dev(sec(other_x(k), c), e, t), device_id_type=MESH,
        )

    def pair_sum(i, xx, n):
        mine = part[i, group_rows(sec(xx, c)), span(n, ft)].astype(jnp.float32)
        return mine + pair_in[i, xx, :, span(n, ft)].astype(jnp.float32)

    def cross(i):
        for xx in range(xs):
            pair_copy(i, xx).wait_recv()
        for k in range(1, xs):

            @pl.loop(0, feats // ft)
            def _(n):
                cross_out[i, k - 1, :, span(n, ft)] = pair_sum(i, other_x(k), n).astype(jnp.bfloat16)

            cross_copy(i, k).start()

    def back_copy(i):
        return pltpu.make_async_remote_copy(
            back_out.at[i], back_in.at[group_rows(e)], back_s.at[i], back_r.at[e],
            device_id=dev(s, source(i), t), device_id_type=MESH,
        )

    own_back = pltpu.make_async_copy(back_out.at[0], back_in.at[group_rows(e)], back_r.at[e])

    def finish(i):
        for k in range(1, xs):
            cross_copy(i, k).wait_recv()

        @pl.loop(0, feats // ft)
        def _(n):
            total = pair_sum(i, x, n)
            for k in range(1, xs):
                total += cross_in[i, k - 1, :, span(n, ft)].astype(jnp.float32)
            back_out[i, :, span(n, ft)] = total.astype(jnp.bfloat16)

        @pl.when(i == 0)
        def _():
            own_back.start()

        @pl.when(i > 0)
        def _():
            back_copy(i).start()

        for xx in range(xs):
            for tt in range(tensors):
                core_copy(i, xx, tt).wait_send()
            pair_copy(i, xx).wait_send()
        for k in range(1, xs):
            px_copy(i, k).wait_send()
            cross_copy(i, k).wait_send()
        for k in range(1, tensors):
            pt_copy(i, k).wait_send()
            hid_copy(i, k).wait_send()
        for kx in range(1, xs):
            for kt in range(1, tensors):
                relay_t_copy(i, kx, kt).wait_send()

    stages = (push, relay, expand, contract, cross, finish)

    @pl.loop(0, experts + len(stages) - 1)
    def _(step):
        for lag, stage in enumerate(stages):

            @pl.when(jnp.logical_and(step >= lag, step < experts + lag))
            def _():
                stage(step - lag)

    own_back.wait()
    for k in range(1, tensors):
        stats_copy(k).wait_send()
    for k in range(1, experts):
        out_copy(k).wait_send()
        back_copy(k).wait_send()
        pltpu.make_async_remote_copy(
            back_out.at[k], back_in.at[group_rows(source(k))], back_s.at[k], back_r.at[source(k)],
            device_id=dev(s, source(k), t), device_id_type=MESH,
        ).wait_recv()

    @pl.loop(0, feats // ft)
    def _(n):
        out_ref[:, span(n, ft)] = jnp.dot(
            placing_ref[...], back_in[:, span(n, ft)], preferred_element_type=jnp.float32
        ).astype(jnp.bfloat16)


def on_device(sections, experts, tensors, tokens, norm_gain, router, expert_ids, gate_proj, up_proj, down_proj):
    rows, feats = tokens.shape
    cap = 2 * rows // experts
    width, units = gate_proj.shape[1:]
    depth = down_proj.shape[1]
    group = sections * cap
    xs = sections // CORES
    bf16 = jnp.bfloat16
    dma = pltpu.SemaphoreType.DMA
    vmem = pl.BlockSpec(memory_space=pltpu.VMEM)
    anywhere = pl.BlockSpec(memory_space=pl.ANY)
    router = jnp.pad(router, ((0, 0), (0, LANES - router.shape[1])))
    return pl.pallas_call(
        functools.partial(sublayer, sections, experts, tensors),
        out_shape=jax.ShapeDtypeStruct((rows, feats), bf16),
        in_specs=[vmem] * 4 + [anywhere] * 3,
        out_specs=vmem,
        scratch_shapes=[
            pltpu.VMEM((width, units), bf16),
            pltpu.VMEM((width, units), bf16),
            pltpu.VMEM((depth, feats), bf16),
            pltpu.VMEM((tensors, rows, LANES), jnp.float32),
            pltpu.VMEM((rows, experts * cap), bf16),
            pltpu.VMEM((experts * cap, feats), bf16),
            pltpu.VMEM((experts, group, width), bf16),
            pltpu.VMEM((experts, group, depth), bf16),
            pltpu.VMEM((experts, group, feats), bf16),
            pltpu.VMEM((experts, xs, cap, feats), bf16),
            pltpu.VMEM((experts, max(1, xs - 1), cap, feats), bf16),
            pltpu.VMEM((experts, max(1, xs - 1), cap, feats), bf16),
            pltpu.VMEM((experts, cap, feats), bf16),
            pltpu.VMEM((experts * cap, feats), bf16),
            dma((3,)),
            dma((tensors,)),
            dma((tensors,)),
            dma((experts,)),
            dma((experts, sections, tensors)),
            dma((experts, xs, tensors)),
            dma((experts, xs, tensors)),
            dma((experts, xs)),
            dma((experts, tensors)),
            dma((experts, tensors)),
            dma((experts, tensors)),
            dma((experts, xs)),
            dma((experts, xs)),
            dma((experts, xs)),
            dma((experts, xs)),
            dma((experts,)),
            dma((experts,)),
        ],
        compiler_params=pltpu.CompilerParams(
            collective_id=0, has_side_effects=True, vmem_limit_bytes=62 * 1024 * 1024
        ),
    )(tokens, norm_gain.reshape(1, feats), router, expert_ids, gate_proj, up_proj, down_proj)


def solution(mesh):
    in_specs = (
        P(("section", "expert"), "tensor"),
        P("tensor"),
        P("tensor", None),
        P(("section", "expert"), None),
        P("expert", None, ("section", "tensor")),
        P("expert", None, ("section", "tensor")),
        P("expert", "section", "tensor"),
    )
    body = functools.partial(on_device, *[mesh.shape[axis] for axis in ("section", "expert", "tensor")])
    return jax.shard_map(
        body, mesh=mesh, in_specs=in_specs, out_specs=P(("section", "expert"), "tensor"), check_vma=False
    )
```

```python
import functools

import jax
import jax.numpy as jnp
from jax import lax
from jax.experimental import pallas as pl
from jax.experimental.pallas import tpu as pltpu
from jax.sharding import PartitionSpec as P

EPSILON = 1e-05
CORES = 2
LANES = 128
HALVES = 2
MESH = pl.DeviceIdType.MESH


def tile_of(width):
    for tile in (512, 256, 128):
        if width % tile == 0:
            return tile
    return width


def sublayer(
    sections, experts, tensors, tokens_ref, gain_ref, router_ref, ids_ref, gate_hbm, up_hbm, down_hbm,
    out_ref, gate_w, up_w, down_w, stats, placing_ref, outgoing, piece, hidden, part, pair_in, cross_out,
    cross_in, back_out, back_in, weight_sem, stats_s, stats_r, out_s, piece_r, core_s, relay_s, px_s,
    pt_s, hid_s, hid_r, pair_s, pair_r, cross_s, cross_r, back_s, back_r,
):
    s, e, t = lax.axis_index("section"), lax.axis_index("expert"), lax.axis_index("tensor")
    x, c = lax.div(s, CORES), lax.rem(s, CORES)
    xs = sections // CORES
    rows, feats = tokens_ref.shape
    width = gate_hbm.shape[1]
    units = gate_hbm.shape[2]
    groups = piece.shape[0]
    halves = groups // experts
    cap = outgoing.shape[0] // groups
    slots = cap * halves
    partner = s + 1 - 2 * c

    def other_x(k):
        return lax.rem(x + k, xs)

    def other_t(k):
        return lax.rem(t + k, tensors)

    def sec(xx, cc):
        return xx * CORES + cc

    def dev(ss, ee, tt):
        return {"section": ss, "expert": ee, "tensor": tt}

    barrier = pltpu.get_barrier_semaphore()
    peers = [dev(partner, e, t)]
    peers += [dev(sec(other_x(k), c), e, t) for k in range(1, xs)]
    peers += [dev(s, e, other_t(k)) for k in range(1, tensors)]
    peers += [dev(s, lax.rem(e + k, experts), t) for k in range(1, experts)]
    for peer in peers:
        pl.semaphore_signal(barrier, inc=1, device_id=peer, device_id_type=MESH)

    loads = [
        pltpu.make_async_copy(gate_hbm.at[0], gate_w, weight_sem.at[0]),
        pltpu.make_async_copy(up_hbm.at[0], up_w, weight_sem.at[1]),
        pltpu.make_async_copy(down_hbm.at[0], down_w, weight_sem.at[2]),
    ]
    for load in loads:
        load.start()

    ft = tile_of(feats)

    def span(n, tile):
        return pl.ds(pl.multiple_of(n * tile, LANES), tile)

    def gather_stats(n, carry):
        squares, logits = carry
        values = tokens_ref[:, span(n, ft)].astype(jnp.float32)
        scaled = (values * gain_ref[span(n, ft)][None, :]).astype(jnp.bfloat16)
        logits += lax.dot_general(
            scaled, router_ref[:, span(n, ft)], (((1,), (1,)), ((), ())),
            preferred_element_type=jnp.float32,
        )
        return squares + jnp.sum(values * values, axis=1, keepdims=True), logits

    squares, logits = lax.fori_loop(
        0, feats // ft, gather_stats,
        (jnp.zeros((rows, 1), jnp.float32), jnp.zeros((rows, experts), jnp.float32)),
    )
    lane = lax.broadcasted_iota(jnp.int32, (rows, LANES), 1)
    stats[t] = jnp.where(lane == experts, squares, 0.0)
    stats[t, :, 0:experts] = logits
    pl.semaphore_wait(barrier, len(peers))

    def stats_copy(k):
        return pltpu.make_async_remote_copy(
            stats.at[t], stats.at[t], stats_s.at[k], stats_r.at[t],
            device_id=dev(s, e, other_t(k)), device_id_type=MESH,
        )

    for k in range(1, tensors):
        stats_copy(k).start()

    across = lax.broadcasted_iota(jnp.int32, (rows, rows), 1)
    down = lax.broadcasted_iota(jnp.int32, (rows, rows), 0)
    chosen = jnp.sum(jnp.where(across == down, ids_ref[...].astype(jnp.float32), 0.0), axis=1, keepdims=True)
    chosen = chosen.astype(jnp.int32)
    member = chosen == lane
    member_f = jnp.where(member, 1.0, 0.0).astype(jnp.float32)
    before = across < down
    earlier = jnp.dot(
        jnp.where(before, 1.0, 0.0).astype(jnp.bfloat16), member_f.astype(jnp.bfloat16),
        preferred_element_type=jnp.float32,
    )
    slot = jnp.sum(earlier * member_f, axis=1, keepdims=True)
    placed = chosen.astype(jnp.float32) * slots + slot
    places = lax.broadcasted_iota(jnp.int32, (rows, experts * slots), 1).astype(jnp.float32)
    placing_ref[...] = jnp.where(placed == places, 1.0, 0.0).astype(jnp.bfloat16)

    for k in range(1, tensors):
        pltpu.make_async_remote_copy(
            stats.at[t], stats.at[other_t(k)], stats_s.at[k], stats_r.at[other_t(k)],
            device_id=dev(s, e, other_t(k)), device_id_type=MESH,
        ).wait_recv()
    total = stats[0]
    for k in range(1, tensors):
        total += stats[k]
    squares = jnp.sum(jnp.where(lane == experts, total, 0.0), axis=1, keepdims=True)
    inverse = lax.rsqrt(squares / width + EPSILON)
    score = jax.nn.sigmoid(jnp.sum(total * member_f, axis=1, keepdims=True) * inverse)

    @pl.loop(0, feats // ft)
    def _(n):
        values = tokens_ref[:, span(n, ft)].astype(jnp.float32)
        normed = (values * inverse * gain_ref[span(n, ft)][None, :]).astype(jnp.bfloat16)
        routed = (normed.astype(jnp.float32) * score).astype(jnp.bfloat16)
        outgoing[:, span(n, ft)] = lax.dot_general(
            placing_ref[...], routed, (((0,), (0,)), ((), ())), preferred_element_type=jnp.float32
        ).astype(jnp.bfloat16)

    def group_rows(index):
        return pl.ds(pl.multiple_of(index * cap, cap), cap)

    def block(z, ss, tt):
        return piece.at[z, group_rows(ss), pl.ds(pl.multiple_of(tt * feats, LANES), feats)]

    def chunk_copy(z, ss, tt, send_sem, to):
        return pltpu.make_async_remote_copy(
            block(z, ss, tt), block(z, ss, tt), send_sem, piece_r.at[z, ss, tt],
            device_id=to, device_id_type=MESH,
        )

    def out_copy(i):
        target = lax.rem(e + lax.div(i, halves), experts)
        h = lax.rem(i, halves)
        return pltpu.make_async_remote_copy(
            outgoing.at[group_rows(target * halves + h)], block(e * halves + h, s, t), out_s.at[i],
            piece_r.at[e * halves + h, s, t],
            device_id=dev(s, target, t), device_id_type=MESH,
        )

    for h in range(halves):
        z = e * halves + h
        pltpu.make_async_copy(outgoing.at[group_rows(z)], block(z, s, t), piece_r.at[z, s, t]).start()

    @pl.loop(halves, groups)
    def _(i):
        out_copy(i).start()

    def owner(i):
        return lax.rem(e + experts - lax.div(i, halves), experts)

    def source(i):
        return owner(i) * halves + lax.rem(i, halves)

    to_partner = dev(partner, e, t)

    def arrived(z, ss, tt):
        chunk_copy(z, ss, tt, core_s.at[0, 0, 0], to_partner).wait_recv()

    def core_copy(i, xx, tt):
        return chunk_copy(source(i), sec(xx, c), tt, core_s.at[i, xx, tt], to_partner)

    def px_copy(i, k):
        return chunk_copy(source(i), s, t, px_s.at[i, k], dev(sec(other_x(k), c), e, t))

    def pt_copy(i, k):
        return chunk_copy(source(i), s, t, pt_s.at[i, k], dev(s, e, other_t(k)))

    def relay_t_copy(i, kx, kt):
        return chunk_copy(
            source(i), sec(other_x(kx), c), t, relay_s.at[i, kx, kt], dev(s, e, other_t(kt))
        )

    def relay_x_copy(i, kx, kt):
        return chunk_copy(
            source(i), s, other_t(kt), relay_s.at[i, kx, kt], dev(sec(other_x(kx), c), e, t)
        )

    def push(i):
        arrived(source(i), s, t)
        for k in range(1, xs):
            px_copy(i, k).start()
        for k in range(1, tensors):
            pt_copy(i, k).start()
        core_copy(i, x, t).start()

    def relay(i):
        even = lax.rem(i, 2) == 0
        for kx in range(1, xs):
            arrived(source(i), sec(other_x(kx), c), t)

            @pl.when(even)
            def _():
                for kt in range(1, tensors):
                    relay_t_copy(i, kx, kt).start()

            core_copy(i, other_x(kx), t).start()
        for kt in range(1, tensors):
            arrived(source(i), s, other_t(kt))

            @pl.when(jnp.logical_not(even))
            def _():
                for kx in range(1, xs):
                    relay_x_copy(i, kx, kt).start()

            core_copy(i, x, other_t(kt)).start()

    ut = min(256, units)

    def hid_block(i, tt, n):
        return hidden.at[i, :, pl.ds(pl.multiple_of(tt * units + n * ut, LANES), ut)]

    def hid_copy(i, k, n):
        return pltpu.make_async_remote_copy(
            hid_block(i, t, n), hid_block(i, t, n), hid_s.at[i, k, n], hid_r.at[i, t, n],
            device_id=dev(s, e, other_t(k)), device_id_type=MESH,
        )


    def expand(i):
        z = source(i)
        for kx in range(1, xs):
            for kt in range(1, tensors):
                arrived(z, sec(other_x(kx), c), other_t(kt))
                core_copy(i, other_x(kx), other_t(kt)).start()
        for xx in range(xs):
            for tt in range(tensors):
                arrived(z, sec(xx, 1 - c), tt)

        @pl.when(i == 0)
        def _():
            loads[0].wait()
            loads[1].wait()
            loads[2].wait()

        @pl.loop(0, units // ut)
        def _(n):
            gate = jnp.dot(piece[z], gate_w[:, span(n, ut)], preferred_element_type=jnp.float32)
            upper = jnp.dot(piece[z], up_w[:, span(n, ut)], preferred_element_type=jnp.float32)
            hidden[i, :, pl.ds(pl.multiple_of(t * units + n * ut, LANES), ut)] = (
                jax.nn.silu(gate) * upper
            ).astype(jnp.bfloat16)
            for k in range(1, tensors):
                hid_copy(i, k, n).start()

    def pair_copy(i, xx, n):
        return pltpu.make_async_remote_copy(
            part.at[i, group_rows(sec(xx, 1 - c)), span(n, ft)], pair_in.at[i, xx, :, span(n, ft)],
            pair_s.at[i, xx, n], pair_r.at[i, xx, n],
            device_id=to_partner, device_id_type=MESH,
        )

    def contract(i):
        for k in range(1, tensors):
            for n in range(units // ut):
                pltpu.make_async_remote_copy(
                    hid_block(i, t, n), hid_block(i, other_t(k), n), hid_s.at[i, k, n],
                    hid_r.at[i, other_t(k), n], device_id=dev(s, e, other_t(k)), device_id_type=MESH,
                ).wait_recv()

        @pl.loop(0, feats // ft)
        def _(n):
            part[i, :, span(n, ft)] = jnp.dot(
                hidden[i], down_w[:, span(n, ft)], preferred_element_type=jnp.float32
            ).astype(jnp.bfloat16)
            for xx in range(xs):
                pair_copy(i, xx, n).start()

    def cross_copy(i, k, n):
        return pltpu.make_async_remote_copy(
            cross_out.at[i, k - 1, :, span(n, ft)], cross_in.at[i, k - 1, :, span(n, ft)],
            cross_s.at[i, k, n], cross_r.at[i, k, n],
            device_id=dev(sec(other_x(k), c), e, t), device_id_type=MESH,
        )

    def pair_sum(i, xx, n):
        mine = part[i, group_rows(sec(xx, c)), span(n, ft)].astype(jnp.float32)
        return mine + pair_in[i, xx, :, span(n, ft)].astype(jnp.float32)

    def cross(i):
        @pl.loop(0, feats // ft)
        def _(n):
            for xx in range(xs):
                pair_copy(i, xx, n).wait_recv()
            for k in range(1, xs):
                cross_out[i, k - 1, :, span(n, ft)] = pair_sum(i, other_x(k), n).astype(jnp.bfloat16)
                cross_copy(i, k, n).start()

    def back_copy(i, n):
        return pltpu.make_async_remote_copy(
            back_out.at[i, :, span(n, ft)], back_in.at[group_rows(e * halves + lax.rem(i, halves)), span(n, ft)],
            back_s.at[i, n], back_r.at[e * halves + lax.rem(i, halves), n],
            device_id=dev(s, owner(i), t), device_id_type=MESH,
        )

    def own_back(i, n):
        return pltpu.make_async_copy(
            back_out.at[i, :, span(n, ft)], back_in.at[group_rows(e * halves + i), span(n, ft)],
            back_r.at[e * halves + i, n],
        )

    def finish(i):
        @pl.loop(0, feats // ft)
        def _(n):
            for k in range(1, xs):
                cross_copy(i, k, n).wait_recv()
            total = pair_sum(i, x, n)
            for k in range(1, xs):
                total += cross_in[i, k - 1, :, span(n, ft)].astype(jnp.float32)
            back_out[i, :, span(n, ft)] = total.astype(jnp.bfloat16)

            @pl.when(i < halves)
            def _():
                own_back(i, n).start()

            @pl.when(i >= halves)
            def _():
                back_copy(i, n).start()

    def settle(i):
        for xx in range(xs):
            for tt in range(tensors):
                core_copy(i, xx, tt).wait_send()
        for k in range(1, xs):
            px_copy(i, k).wait_send()
        for k in range(1, tensors):
            pt_copy(i, k).wait_send()
            for n in range(units // ut):
                hid_copy(i, k, n).wait_send()
        for kx in range(1, xs):
            for kt in range(1, tensors):
                relay_t_copy(i, kx, kt).wait_send()
        for n in range(feats // ft):
            for xx in range(xs):
                pair_copy(i, xx, n).wait_send()
            for k in range(1, xs):
                cross_copy(i, k, n).wait_send()

    stages = ((1, relay), (0, push), (2, expand), (3, contract), (4, cross), (5, finish))

    @pl.loop(0, groups + len(stages) - 1)
    def _(step):
        for lag, stage in stages:

            @pl.when(jnp.logical_and(step >= lag, step < groups + lag))
            def _():
                stage(step - lag)

    @pl.loop(0, groups)
    def _(i):
        settle(i)

    @pl.loop(0, halves)
    def _(i):
        for n in range(feats // ft):
            own_back(i, n).wait()

    for k in range(1, tensors):
        stats_copy(k).wait_send()

    @pl.loop(halves, groups)
    def _(i):
        out_copy(i).wait_send()
        for n in range(feats // ft):
            back_copy(i, n).wait_send()
            pltpu.make_async_remote_copy(
                back_out.at[i, :, span(n, ft)], back_in.at[group_rows(source(i)), span(n, ft)],
                back_s.at[i, n], back_r.at[source(i), n], device_id=dev(s, owner(i), t), device_id_type=MESH,
            ).wait_recv()

    @pl.loop(0, feats // ft)
    def _(n):
        out_ref[:, span(n, ft)] = jnp.dot(
            placing_ref[...], back_in[:, span(n, ft)], preferred_element_type=jnp.float32
        ).astype(jnp.bfloat16)


def on_device(sections, experts, tensors, tokens, norm_gain, router, expert_ids, gate_proj, up_proj, down_proj):
    rows, feats = tokens.shape
    slots = 2 * rows // experts
    halves = HALVES if slots % (16 * HALVES) == 0 else 1
    cap = slots // halves
    groups = experts * halves
    width, units = gate_proj.shape[1:]
    depth = down_proj.shape[1]
    group = sections * cap
    xs = sections // CORES
    bf16 = jnp.bfloat16
    dma = pltpu.SemaphoreType.DMA
    vmem = pl.BlockSpec(memory_space=pltpu.VMEM)
    anywhere = pl.BlockSpec(memory_space=pl.ANY)
    pieces = feats // tile_of(feats)
    tiles = units // min(256, units)
    return pl.pallas_call(
        functools.partial(sublayer, sections, experts, tensors),
        out_shape=jax.ShapeDtypeStruct((rows, feats), bf16),
        in_specs=[vmem] * 4 + [anywhere] * 3,
        out_specs=vmem,
        scratch_shapes=[
            pltpu.VMEM((width, units), bf16),
            pltpu.VMEM((width, units), bf16),
            pltpu.VMEM((depth, feats), bf16),
            pltpu.VMEM((tensors, rows, LANES), jnp.float32),
            pltpu.VMEM((rows, groups * cap), bf16),
            pltpu.VMEM((groups * cap, feats), bf16),
            pltpu.VMEM((groups, group, width), bf16),
            pltpu.VMEM((groups, group, depth), bf16),
            pltpu.VMEM((groups, group, feats), bf16),
            pltpu.VMEM((groups, xs, cap, feats), bf16),
            pltpu.VMEM((groups, max(1, xs - 1), cap, feats), bf16),
            pltpu.VMEM((groups, max(1, xs - 1), cap, feats), bf16),
            pltpu.VMEM((groups, cap, feats), bf16),
            pltpu.VMEM((groups * cap, feats), bf16),
            dma((3,)),
            dma((tensors,)),
            dma((tensors,)),
            dma((groups,)),
            dma((groups, sections, tensors)),
            dma((groups, xs, tensors)),
            dma((groups, xs, tensors)),
            dma((groups, xs)),
            dma((groups, tensors)),
            dma((groups, tensors, tiles)),
            dma((groups, tensors, tiles)),
            dma((groups, xs, pieces)),
            dma((groups, xs, pieces)),
            dma((groups, xs, pieces)),
            dma((groups, xs, pieces)),
            dma((groups, pieces)),
            dma((groups, pieces)),
        ],
        compiler_params=pltpu.CompilerParams(
            collective_id=0, has_side_effects=True, vmem_limit_bytes=62 * 1024 * 1024
        ),
    )(tokens, norm_gain, router.T, expert_ids.reshape(1, rows), gate_proj, up_proj, down_proj)


def solution(mesh):
    in_specs = (
        P(("section", "expert"), "tensor"),
        P("tensor"),
        P("tensor", None),
        P(("section", "expert"), None),
        P("expert", None, ("section", "tensor")),
        P("expert", None, ("section", "tensor")),
        P("expert", "section", "tensor"),
    )
    body = functools.partial(on_device, *[mesh.shape[axis] for axis in ("section", "expert", "tensor")])
    return jax.shard_map(
        body, mesh=mesh, in_specs=in_specs, out_specs=P(("section", "expert"), "tensor"), check_vma=False
    )
```

```python
import functools

import jax
import jax.numpy as jnp
from jax import lax
from jax.experimental import pallas as pl
from jax.experimental.pallas import tpu as pltpu
from jax.sharding import PartitionSpec as P

EPSILON = 1e-05
CORES = 2
LANES = 128
HALVES = 2
MESH = pl.DeviceIdType.MESH


def tile_of(width):
    for tile in (1280, 640, 512, 256, 128):
        if width % tile == 0:
            return tile
    return width


def sublayer(
    sections, experts, tensors, tokens_ref, gain_ref, router_ref, ids_ref, gate_hbm, up_hbm, down_hbm,
    out_ref, gate_w, up_w, down_w, stats, placing_ref, outgoing, piece, hidden, part, pair_in, cross_out,
    cross_in, back_out, back_in, weight_sem, stats_s, stats_r, out_s, piece_r, core_s, relay_s, px_s,
    pt_s, hid_s, hid_r, pair_s, pair_r, cross_s, cross_r, back_s, back_r,
):
    s, e, t = lax.axis_index("section"), lax.axis_index("expert"), lax.axis_index("tensor")
    x, c = lax.div(s, CORES), lax.rem(s, CORES)
    xs = sections // CORES
    rows, feats = tokens_ref.shape
    width = gate_hbm.shape[1]
    units = gate_hbm.shape[2]
    groups = piece.shape[0]
    halves = groups // experts
    cap = outgoing.shape[0] // groups
    slots = cap * halves
    partner = s + 1 - 2 * c

    def other_x(k):
        return lax.rem(x + k, xs)

    def other_t(k):
        return lax.rem(t + k, tensors)

    def sec(xx, cc):
        return xx * CORES + cc

    def dev(ss, ee, tt):
        return {"section": ss, "expert": ee, "tensor": tt}

    barrier = pltpu.get_barrier_semaphore()
    peers = [dev(partner, e, t)]
    peers += [dev(sec(other_x(k), c), e, t) for k in range(1, xs)]
    peers += [dev(s, e, other_t(k)) for k in range(1, tensors)]
    peers += [dev(s, lax.rem(e + k, experts), t) for k in range(1, experts)]
    for peer in peers:
        pl.semaphore_signal(barrier, inc=1, device_id=peer, device_id_type=MESH)

    loads = [
        pltpu.make_async_copy(gate_hbm.at[0], gate_w, weight_sem.at[0]),
        pltpu.make_async_copy(up_hbm.at[0], up_w, weight_sem.at[1]),
        pltpu.make_async_copy(down_hbm.at[0], down_w, weight_sem.at[2]),
    ]
    for load in loads:
        load.start()

    ft = tile_of(feats)

    def span(n, tile):
        return pl.ds(pl.multiple_of(n * tile, LANES), tile)

    def gather_stats(n, carry):
        squares, logits = carry
        values = tokens_ref[:, span(n, ft)].astype(jnp.float32)
        scaled = (values * gain_ref[span(n, ft)][None, :]).astype(jnp.bfloat16)
        logits += lax.dot_general(
            scaled, router_ref[:, span(n, ft)], (((1,), (1,)), ((), ())),
            preferred_element_type=jnp.float32,
        )
        return squares + jnp.sum(values * values, axis=1, keepdims=True), logits

    squares, logits = lax.fori_loop(
        0, feats // ft, gather_stats,
        (jnp.zeros((rows, 1), jnp.float32), jnp.zeros((rows, experts), jnp.float32)),
    )
    lane = lax.broadcasted_iota(jnp.int32, (rows, LANES), 1)
    stats[t] = jnp.where(lane == experts, squares, 0.0)
    stats[t, :, 0:experts] = logits
    pl.semaphore_wait(barrier, len(peers))

    def stats_copy(k):
        return pltpu.make_async_remote_copy(
            stats.at[t], stats.at[t], stats_s.at[k], stats_r.at[t],
            device_id=dev(s, e, other_t(k)), device_id_type=MESH,
        )

    for k in range(1, tensors):
        stats_copy(k).start()

    across = lax.broadcasted_iota(jnp.int32, (rows, rows), 1)
    down = lax.broadcasted_iota(jnp.int32, (rows, rows), 0)
    chosen = jnp.sum(jnp.where(across == down, ids_ref[...].astype(jnp.float32), 0.0), axis=1, keepdims=True)
    chosen = chosen.astype(jnp.int32)
    member = chosen == lane
    member_f = jnp.where(member, 1.0, 0.0).astype(jnp.float32)
    before = across < down
    earlier = jnp.dot(
        jnp.where(before, 1.0, 0.0).astype(jnp.bfloat16), member_f.astype(jnp.bfloat16),
        preferred_element_type=jnp.float32,
    )
    slot = jnp.sum(earlier * member_f, axis=1, keepdims=True)
    placed = chosen.astype(jnp.float32) * slots + slot
    places = lax.broadcasted_iota(jnp.int32, (rows, experts * slots), 1).astype(jnp.float32)
    placing_ref[...] = jnp.where(placed == places, 1.0, 0.0).astype(jnp.bfloat16)

    for k in range(1, tensors):
        pltpu.make_async_remote_copy(
            stats.at[t], stats.at[other_t(k)], stats_s.at[k], stats_r.at[other_t(k)],
            device_id=dev(s, e, other_t(k)), device_id_type=MESH,
        ).wait_recv()
    total = stats[0]
    for k in range(1, tensors):
        total += stats[k]
    squares = jnp.sum(jnp.where(lane == experts, total, 0.0), axis=1, keepdims=True)
    inverse = lax.rsqrt(squares / width + EPSILON)
    score = jax.nn.sigmoid(jnp.sum(total * member_f, axis=1, keepdims=True) * inverse)

    @pl.loop(0, feats // ft)
    def _(n):
        values = tokens_ref[:, span(n, ft)].astype(jnp.float32)
        normed = (values * inverse * gain_ref[span(n, ft)][None, :]).astype(jnp.bfloat16)
        routed = (normed.astype(jnp.float32) * score).astype(jnp.bfloat16)
        outgoing[:, span(n, ft)] = lax.dot_general(
            placing_ref[...], routed, (((0,), (0,)), ((), ())), preferred_element_type=jnp.float32
        ).astype(jnp.bfloat16)

    def group_rows(index):
        return pl.ds(pl.multiple_of(index * cap, cap), cap)

    def block(z, ss, tt):
        return piece.at[z, group_rows(ss), pl.ds(pl.multiple_of(tt * feats, LANES), feats)]

    def chunk_copy(z, ss, tt, send_sem, to):
        return pltpu.make_async_remote_copy(
            block(z, ss, tt), block(z, ss, tt), send_sem, piece_r.at[z, ss, tt],
            device_id=to, device_id_type=MESH,
        )

    def out_copy(i):
        target = lax.rem(e + lax.div(i, halves), experts)
        h = lax.rem(i, halves)
        return pltpu.make_async_remote_copy(
            outgoing.at[group_rows(target * halves + h)], block(e * halves + h, s, t), out_s.at[i],
            piece_r.at[e * halves + h, s, t],
            device_id=dev(s, target, t), device_id_type=MESH,
        )

    for h in range(halves):
        z = e * halves + h
        pltpu.make_async_copy(outgoing.at[group_rows(z)], block(z, s, t), piece_r.at[z, s, t]).start()

    @pl.loop(halves, groups)
    def _(i):
        out_copy(i).start()

    def owner(i):
        return lax.rem(e + experts - lax.div(i, halves), experts)

    def source(i):
        return owner(i) * halves + lax.rem(i, halves)

    to_partner = dev(partner, e, t)

    def arrived(z, ss, tt):
        chunk_copy(z, ss, tt, core_s.at[0, 0, 0], to_partner).wait_recv()

    def core_copy(i, xx, tt):
        return chunk_copy(source(i), sec(xx, c), tt, core_s.at[i, xx, tt], to_partner)

    def px_copy(i, k):
        return chunk_copy(source(i), s, t, px_s.at[i, k], dev(sec(other_x(k), c), e, t))

    def pt_copy(i, k):
        return chunk_copy(source(i), s, t, pt_s.at[i, k], dev(s, e, other_t(k)))

    def relay_t_copy(i, kx, kt):
        return chunk_copy(
            source(i), sec(other_x(kx), c), t, relay_s.at[i, kx, kt], dev(s, e, other_t(kt))
        )

    def relay_x_copy(i, kx, kt):
        return chunk_copy(
            source(i), s, other_t(kt), relay_s.at[i, kx, kt], dev(sec(other_x(kx), c), e, t)
        )

    def push(i):
        arrived(source(i), s, t)
        for k in range(1, xs):
            px_copy(i, k).start()
        for k in range(1, tensors):
            pt_copy(i, k).start()
        core_copy(i, x, t).start()

    def relay(i):
        even = lax.rem(i, 2) == 0
        for kx in range(1, xs):
            arrived(source(i), sec(other_x(kx), c), t)

            @pl.when(even)
            def _():
                for kt in range(1, tensors):
                    relay_t_copy(i, kx, kt).start()

            core_copy(i, other_x(kx), t).start()
        for kt in range(1, tensors):
            arrived(source(i), s, other_t(kt))

            @pl.when(jnp.logical_not(even))
            def _():
                for kx in range(1, xs):
                    relay_x_copy(i, kx, kt).start()

            core_copy(i, x, other_t(kt)).start()

    ut = min(256, units)

    def hid_block(i, tt, n):
        return hidden.at[i, :, pl.ds(pl.multiple_of(tt * units + n * ut, LANES), ut)]

    def hid_copy(i, k, n):
        return pltpu.make_async_remote_copy(
            hid_block(i, t, n), hid_block(i, t, n), hid_s.at[i, k, n], hid_r.at[i, t, n],
            device_id=dev(s, e, other_t(k)), device_id_type=MESH,
        )


    def expand(i):
        z = source(i)
        for kx in range(1, xs):
            for kt in range(1, tensors):
                arrived(z, sec(other_x(kx), c), other_t(kt))
                core_copy(i, other_x(kx), other_t(kt)).start()
        for xx in range(xs):
            for tt in range(tensors):
                arrived(z, sec(xx, 1 - c), tt)

        @pl.when(i == 0)
        def _():
            loads[0].wait()
            loads[1].wait()
            loads[2].wait()

        @pl.loop(0, units // ut)
        def _(n):
            gate = jnp.dot(piece[z], gate_w[:, span(n, ut)], preferred_element_type=jnp.float32)
            upper = jnp.dot(piece[z], up_w[:, span(n, ut)], preferred_element_type=jnp.float32)
            hidden[i, :, pl.ds(pl.multiple_of(t * units + n * ut, LANES), ut)] = (
                jax.nn.silu(gate) * upper
            ).astype(jnp.bfloat16)
            for k in range(1, tensors):
                hid_copy(i, k, n).start()

    def pair_copy(i, xx, n):
        return pltpu.make_async_remote_copy(
            part.at[i, group_rows(sec(xx, 1 - c)), span(n, ft)], pair_in.at[i, xx, :, span(n, ft)],
            pair_s.at[i, xx, n], pair_r.at[i, xx, n],
            device_id=to_partner, device_id_type=MESH,
        )

    def contract(i):
        for k in range(1, tensors):
            for n in range(units // ut):
                pltpu.make_async_remote_copy(
                    hid_block(i, t, n), hid_block(i, other_t(k), n), hid_s.at[i, k, n],
                    hid_r.at[i, other_t(k), n], device_id=dev(s, e, other_t(k)), device_id_type=MESH,
                ).wait_recv()

        @pl.loop(0, feats // ft)
        def _(n):
            part[i, :, span(n, ft)] = jnp.dot(
                hidden[i], down_w[:, span(n, ft)], preferred_element_type=jnp.float32
            ).astype(jnp.bfloat16)
            for xx in range(xs):
                pair_copy(i, xx, n).start()

    def cross_copy(i, k, n):
        return pltpu.make_async_remote_copy(
            cross_out.at[i, k - 1, :, span(n, ft)], cross_in.at[i, k - 1, :, span(n, ft)],
            cross_s.at[i, k, n], cross_r.at[i, k, n],
            device_id=dev(sec(other_x(k), c), e, t), device_id_type=MESH,
        )

    def pair_sum(i, xx, n):
        mine = part[i, group_rows(sec(xx, c)), span(n, ft)].astype(jnp.float32)
        return mine + pair_in[i, xx, :, span(n, ft)].astype(jnp.float32)

    def cross(i):
        @pl.loop(0, feats // ft)
        def _(n):
            for xx in range(xs):
                pair_copy(i, xx, n).wait_recv()
            for k in range(1, xs):
                cross_out[i, k - 1, :, span(n, ft)] = pair_sum(i, other_x(k), n).astype(jnp.bfloat16)
                cross_copy(i, k, n).start()

    def back_copy(i, n):
        return pltpu.make_async_remote_copy(
            back_out.at[i, :, span(n, ft)], back_in.at[group_rows(e * halves + lax.rem(i, halves)), span(n, ft)],
            back_s.at[i, n], back_r.at[e * halves + lax.rem(i, halves), n],
            device_id=dev(s, owner(i), t), device_id_type=MESH,
        )

    def own_back(i, n):
        return pltpu.make_async_copy(
            back_out.at[i, :, span(n, ft)], back_in.at[group_rows(e * halves + i), span(n, ft)],
            back_r.at[e * halves + i, n],
        )

    def finish(i):
        @pl.loop(0, feats // ft)
        def _(n):
            for k in range(1, xs):
                cross_copy(i, k, n).wait_recv()
            total = pair_sum(i, x, n)
            for k in range(1, xs):
                total += cross_in[i, k - 1, :, span(n, ft)].astype(jnp.float32)
            back_out[i, :, span(n, ft)] = total.astype(jnp.bfloat16)

            @pl.when(i < halves)
            def _():
                own_back(i, n).start()

            @pl.when(i >= halves)
            def _():
                back_copy(i, n).start()

    def settle(i):
        for xx in range(xs):
            for tt in range(tensors):
                core_copy(i, xx, tt).wait_send()
        for k in range(1, xs):
            px_copy(i, k).wait_send()
        for k in range(1, tensors):
            pt_copy(i, k).wait_send()
            for n in range(units // ut):
                hid_copy(i, k, n).wait_send()
        for kx in range(1, xs):
            for kt in range(1, tensors):
                relay_t_copy(i, kx, kt).wait_send()
        for n in range(feats // ft):
            for xx in range(xs):
                pair_copy(i, xx, n).wait_send()
            for k in range(1, xs):
                cross_copy(i, k, n).wait_send()

    stages = ((1, relay), (0, push), (2, expand), (3, contract), (4, cross), (5, finish))

    @pl.loop(0, groups + len(stages) - 1)
    def _(step):
        for lag, stage in stages:

            @pl.when(jnp.logical_and(step >= lag, step < groups + lag))
            def _():
                stage(step - lag)

    @pl.loop(0, groups)
    def _(i):
        settle(i)

    @pl.loop(0, halves)
    def _(i):
        for n in range(feats // ft):
            own_back(i, n).wait()

    for k in range(1, tensors):
        stats_copy(k).wait_send()

    @pl.loop(halves, groups)
    def _(i):
        out_copy(i).wait_send()
        for n in range(feats // ft):
            back_copy(i, n).wait_send()
            pltpu.make_async_remote_copy(
                back_out.at[i, :, span(n, ft)], back_in.at[group_rows(source(i)), span(n, ft)],
                back_s.at[i, n], back_r.at[source(i), n], device_id=dev(s, owner(i), t), device_id_type=MESH,
            ).wait_recv()

    @pl.loop(0, feats // ft)
    def _(n):
        out_ref[:, span(n, ft)] = jnp.dot(
            placing_ref[...], back_in[:, span(n, ft)], preferred_element_type=jnp.float32
        ).astype(jnp.bfloat16)


def on_device(sections, experts, tensors, tokens, norm_gain, router, expert_ids, gate_proj, up_proj, down_proj):
    rows, feats = tokens.shape
    slots = 2 * rows // experts
    halves = HALVES if slots % (16 * HALVES) == 0 else 1
    cap = slots // halves
    groups = experts * halves
    width, units = gate_proj.shape[1:]
    depth = down_proj.shape[1]
    group = sections * cap
    xs = sections // CORES
    bf16 = jnp.bfloat16
    dma = pltpu.SemaphoreType.DMA
    vmem = pl.BlockSpec(memory_space=pltpu.VMEM)
    anywhere = pl.BlockSpec(memory_space=pl.ANY)
    pieces = feats // tile_of(feats)
    tiles = units // min(256, units)
    return pl.pallas_call(
        functools.partial(sublayer, sections, experts, tensors),
        out_shape=jax.ShapeDtypeStruct((rows, feats), bf16),
        in_specs=[vmem] * 4 + [anywhere] * 3,
        out_specs=vmem,
        scratch_shapes=[
            pltpu.VMEM((width, units), bf16),
            pltpu.VMEM((width, units), bf16),
            pltpu.VMEM((depth, feats), bf16),
            pltpu.VMEM((tensors, rows, LANES), jnp.float32),
            pltpu.VMEM((rows, groups * cap), bf16),
            pltpu.VMEM((groups * cap, feats), bf16),
            pltpu.VMEM((groups, group, width), bf16),
            pltpu.VMEM((groups, group, depth), bf16),
            pltpu.VMEM((groups, group, feats), bf16),
            pltpu.VMEM((groups, xs, cap, feats), bf16),
            pltpu.VMEM((groups, max(1, xs - 1), cap, feats), bf16),
            pltpu.VMEM((groups, max(1, xs - 1), cap, feats), bf16),
            pltpu.VMEM((groups, cap, feats), bf16),
            pltpu.VMEM((groups * cap, feats), bf16),
            dma((3,)),
            dma((tensors,)),
            dma((tensors,)),
            dma((groups,)),
            dma((groups, sections, tensors)),
            dma((groups, xs, tensors)),
            dma((groups, xs, tensors)),
            dma((groups, xs)),
            dma((groups, tensors)),
            dma((groups, tensors, tiles)),
            dma((groups, tensors, tiles)),
            dma((groups, xs, pieces)),
            dma((groups, xs, pieces)),
            dma((groups, xs, pieces)),
            dma((groups, xs, pieces)),
            dma((groups, pieces)),
            dma((groups, pieces)),
        ],
        compiler_params=pltpu.CompilerParams(
            collective_id=0, has_side_effects=True, vmem_limit_bytes=62 * 1024 * 1024
        ),
    )(tokens, norm_gain, router.T, expert_ids.reshape(1, rows), gate_proj, up_proj, down_proj)


def solution(mesh):
    in_specs = (
        P(("section", "expert"), "tensor"),
        P("tensor"),
        P("tensor", None),
        P(("section", "expert"), None),
        P("expert", None, ("section", "tensor")),
        P("expert", None, ("section", "tensor")),
        P("expert", "section", "tensor"),
    )
    body = functools.partial(on_device, *[mesh.shape[axis] for axis in ("section", "expert", "tensor")])
    return jax.shard_map(
        body, mesh=mesh, in_specs=in_specs, out_specs=P(("section", "expert"), "tensor"), check_vma=False
    )
```
